512 devices in a mesh: ep: 128 (over y, z, core), hid: 4 (over x).
Axes of the slice: x: 4, y: 8, z: 8, core: 2. Of those that a mesh axis runs over, the one named last changes fastest.
Arguments:
- attention: bfloat16 [8192, 1536], P('ep', 'hid'), may hold values from -6 to 6
- stream: bfloat16 [8192, 1536], P('ep', 'hid'), may hold values from -16 to 16
- o_weight: bfloat16 [1536, 1536], P('hid'), may hold values from -0.15625 to 0.15625
- routes: int32 [8192, 4], P('ep'), may hold values from 0 to 31, all different within a row; in each aligned block of 64 rows (0 to 63, 64 to 127, ...) at most 16 rows name the same one
- route_weight: float32 [8192, 4], P('ep'), may hold values from 0.1 to 1
- gate_up: bfloat16 [128, 1536, 2, 768], P('ep', None, None, 'hid'), as said below
- down_proj: bfloat16 [128, 768, 1536], P('ep', 'hid'), as said below
- norm_gain: float32 [1536], P('hid'), may hold values from 0.1 to 1.9
Outputs:
- stream_out: bfloat16 [8192, 1536], P('ep', 'hid')
- normed: bfloat16 [8192, 1536], P('ep', 'hid')
The draws below stay inside these ranges and needn't reach their ends.
Inputs may be any that keep to these rules, and one draw needn't show every extreme that they name: `routes`: A row names 4 different experts. In each aligned block of 64 rows (the rows of one index of ep) no expert is named by more than 16 rows, a bound that some block reaches. `gate_up`: slot s holds the weights of expert s mod 32; all slots of one expert are equal. `down_proj`: slot s holds the weights of expert s mod 32; all slots of one expert are equal.
All inputs are finite; a program needn't handle non-finite values.
Results may differ from the reference program's by a relative error of at most 0.019.
Values may be sent and summed in bfloat16 or wider, within the bound.
A program may use at most 64 MiB of HBM per device.

```python
import math
import jax
import jax.numpy as jnp
import numpy as np
from jax import lax

D = 1536
EXPERTS = 32
TOPK = 4
FF = 768
TOK_DEV = 64
ATT = 1536
FQ = 192
MOST = 16
SLOTS = 128
TOKENS = 8192
N_EP = 128


def draw_stream(key, part):
    column = jnp.arange(D, dtype=jnp.float32) / (D - 1)
    column_scale = 0.4 * jnp.power(10.0, column)
    values = jnp.clip(jax.random.normal(key, (TOKENS, D), jnp.float32), -4.0, 4.0) * column_scale[None, :]
    return values.astype(jnp.bfloat16)


def draw_gate_up(key, part):
    shape = (EXPERTS, D, 2, FF)
    values = jax.random.normal(key, shape, jnp.float32)
    values = (values * (1.0 / math.sqrt(D))).astype(jnp.bfloat16)
    return jnp.tile(values, (SLOTS // EXPERTS, 1, 1, 1))


def draw_down_proj(key, part):
    shape = (EXPERTS, FF, D)
    values = jax.random.normal(key, shape, jnp.float32)
    values = (values * (1.0 / math.sqrt(FF))).astype(jnp.bfloat16)
    return jnp.tile(values, (SLOTS // EXPERTS, 1, 1))


def block_levels(stream_key, extent, shards, smallest, high):
    def one(dim, shards_of):
        draws = jax.random.uniform(jax.random.fold_in(jax.random.fold_in(stream_key, 6), dim), (shards_of,), jnp.float32, smallest / len(shards), high / len(shards))
        return jnp.repeat(jnp.exp(draws), extent[dim] // shards_of).reshape((-1,) + (1,) * (len(extent) - dim - 1))

    factor_of = one(*shards[0])
    for cut in shards[1:]:
        factor_of = factor_of * one(*cut)
    return factor_of


def assign_block(rng, own, number, rows, number_of, top, bound, lean):
    sequence = jax.random.permutation(rng, number_of)
    packed, ordinary = load_shares(number_of, rows * top, bound, lean, True), load_shares(number_of, rows * top, bound, lean, False)
    places = jnp.arange(number_of)

    def named(sizes, offset_by):
        used = int((sizes > 0).sum())
        fixed = max(1, used // 4)
        shifted = fixed + (places - fixed + offset_by * (used - fixed)) % max(1, number_of - fixed)
        return jnp.zeros((number_of,), jnp.int32).at[sequence[jnp.where(places < fixed, places, shifted)]].set(jnp.asarray(sizes, jnp.int32))

    sizes = jnp.where(number % 4 == 0, named(packed, number // 4), named(ordinary, number - number // 4 - 1))
    mixed = jax.random.permutation(jax.random.fold_in(own, 3), number_of)
    source_of, taker = mixed[0:number_of // 2 * 2:2], mixed[1:number_of // 2 * 2:2]
    slack = jnp.minimum(sizes[source_of] - 1, bound - sizes[taker]) // 2
    slack = jnp.where((source_of == sequence[0]) | (taker == sequence[0]) | (sizes[taker] == 0), 0, jnp.maximum(slack, 0))
    shifted = jax.random.randint(jax.random.fold_in(own, 4), (number_of // 2,), 0, 1 << 20) % (slack + 1)
    sizes = sizes.at[source_of].add(-shifted).at[taker].add(shifted)
    members = jnp.searchsorted(jnp.cumsum(sizes), jnp.arange(rows * top), side="right").astype(jnp.int32)
    listing = members.reshape(top, rows).T
    listing = listing[jax.random.permutation(jax.random.fold_in(own, 1), rows)]
    offset_by = jax.random.randint(jax.random.fold_in(own, 2), (rows, 1), 0, top)
    return jnp.take_along_axis(listing, (jnp.arange(top)[None, :] + offset_by) % top, axis=1)


def load_shares(amount, total, most, skew, full):
    weights = [(1 << 20) // math.isqrt(rank ** skew) + 1 for rank in range(1, amount + 1)]
    largest = most if full else min(most, max(-(-total // amount), total * weights[0] // sum(weights)))
    least = 1 if total - largest >= amount - 1 else 0
    holding, spare = [largest] + [least] * (amount - 1), total - largest - least * (amount - 1)
    while spare > 0:
        free = [i for i in range(1, amount) if holding[i] < largest] or [i for i in range(1, amount) if holding[i] < most]
        whole, left = sum([weights[i] for i in free]), spare
        for i in free:
            more = min(most - holding[i], max(1, left * weights[i] // whole), spare)
            holding[i] = holding[i] + more
            spare = spare - more
    return np.array(holding)


def normal_values(own_key, shape, spread, bound, cuts=(), held_as=jnp.bfloat16):
    factor_of = block_levels(own_key, shape, cuts, -0.22, 0.18) if cuts else 1.0
    values = jax.random.normal(own_key, shape, jnp.float32) * spread * factor_of
    return jnp.minimum(jnp.maximum(values, -bound), bound).astype(held_as)


def setup_inputs(seed: int = 0) -> dict:
    splits = jax.random.split(jax.random.key(seed), 9)
    attention = normal_values(splits[0], (TOKENS, ATT), 1.0, 6.0, ((0, 128), (1, 4)))
    stream = draw_stream(jax.random.fold_in(splits[8], 71), 0)
    o_weight = normal_values(splits[2], (ATT, D), ATT ** -0.5, 0.15625, ((0, 4),))
    routes_keys = jax.random.split(jax.random.fold_in(splits[3], 1), TOKENS // TOK_DEV)
    routes_turns = jax.random.permutation(jax.random.fold_in(splits[3], 3), TOKENS // TOK_DEV)
    routes = jax.vmap(lambda own, number: assign_block(jax.random.fold_in(splits[3], 2), own, number, TOK_DEV, EXPERTS, TOPK, MOST, 2))(routes_keys, routes_turns).reshape((TOKENS, TOPK))
    route_weight = jnp.clip(0.1 + 0.9 * jax.random.uniform(splits[4], (TOKENS, TOPK), jnp.float32) ** block_levels(splits[4], (TOKENS, TOPK), ((0, 128),), -0.2, 0.2), 0.1, 1.0)
    gate_up = draw_gate_up(jax.random.fold_in(splits[8], 71), 0)
    down_proj = draw_down_proj(jax.random.fold_in(splits[8], 71), 0)
    norm_gain = jnp.clip(1.0 + 0.18 * jax.random.normal(splits[7], (D,), jnp.float32), 0.1, 1.9)
    return dict(attention=attention, stream=stream, o_weight=o_weight, routes=routes, route_weight=route_weight, gate_up=gate_up, down_proj=down_proj, norm_gain=norm_gain)


epsilon = 1e-06

def expert_rows(rows_in, gate_cols, down_rows):
    width = down_rows.shape[0]
    gate_up_out = jnp.dot(rows_in.astype(jnp.float32), gate_cols.astype(jnp.float32), preferred_element_type=jnp.float32)
    hidden = (jax.nn.relu(gate_up_out[:, :width]) * gate_up_out[:, width:]).astype(jnp.bfloat16)
    summed = jnp.zeros((rows_in.shape[0], down_rows.shape[1]), jnp.float32)
    for group_index in range(width // FQ):
        first_unit = group_index * FQ
        group_piece = jnp.dot(hidden[:, first_unit:first_unit + FQ].astype(jnp.float32), down_rows[first_unit:first_unit + FQ].astype(jnp.float32), preferred_element_type=jnp.float32)
        rounded = lax.optimization_barrier(group_piece.astype(jnp.bfloat16))
        summed = summed + rounded.astype(jnp.float32)
    return summed.astype(jnp.bfloat16)

def reference(attention, stream, o_weight, routes, route_weight, gate_up, down_proj, norm_gain):
    projected = jnp.dot(attention.astype(jnp.float32), o_weight.astype(jnp.float32), preferred_element_type=jnp.float32)
    mixed_rows = (stream.astype(jnp.float32) + projected).astype(jnp.bfloat16)
    flat_expert = routes.reshape(-1).astype(jnp.int32)
    flat_count = TOKENS * TOPK
    onehot = (flat_expert[:, None] == jnp.arange(EXPERTS, dtype=jnp.int32)[None, :]).astype(jnp.int32)
    row_rank = lax.optimization_barrier(jnp.sum((jnp.cumsum(onehot, axis=0) - onehot) * onehot, axis=1)).astype(jnp.int32)
    expert_room = N_EP * MOST
    row_table = jnp.full((EXPERTS * expert_room,), flat_count, jnp.int32)
    row_table = row_table.at[flat_expert * expert_room + row_rank].set(jnp.arange(flat_count, dtype=jnp.int32))
    row_table = row_table.reshape(EXPERTS, expert_room)
    padded_rows = jnp.concatenate([mixed_rows, jnp.zeros((1, D), jnp.bfloat16)], axis=0)
    flat_weight = jnp.concatenate([route_weight.reshape(-1).astype(jnp.float32), jnp.zeros((1,), jnp.float32)])

    def one_expert(mixture, inputs):
        expert_index, table_row = inputs
        token_index = (table_row // TOPK).astype(jnp.int32)
        gate_cols = gate_up[expert_index].reshape(D, 2 * FF)
        outputs = expert_rows(padded_rows[token_index], gate_cols, down_proj[expert_index])
        weighted = flat_weight[table_row][:, None] * outputs.astype(jnp.float32)
        return (mixture.at[token_index].add(weighted), None)
    mixture, unused = lax.scan(one_expert, jnp.zeros((TOKENS + 1, D), jnp.float32), (jnp.arange(EXPERTS, dtype=jnp.int32), row_table))
    residual = mixed_rows.astype(jnp.float32) + mixture[:TOKENS]
    rms = lax.optimization_barrier(jnp.mean(residual * residual, axis=1))
    normed = (residual * lax.rsqrt(rms + epsilon)[:, None] * norm_gain.astype(jnp.float32)).astype(jnp.bfloat16)
    return (residual.astype(jnp.bfloat16), normed)
```

```python
import functools

import jax
import jax.numpy as jnp
from jax import lax
from jax.experimental import pallas as pl
from jax.experimental.pallas import tpu as pltpu
from jax.sharding import PartitionSpec as P

EXPERTS = 32
MOST = 16
HID = 4
CHUNKS = 4
EPSILON = 1e-06
BF = jnp.bfloat16
F32 = jnp.float32


def dot(a, b):
    return jnp.dot(a, b, preferred_element_type=F32)


def kernel(
    att_ref, stream_ref, routes_ref, rw_ref, gain_ref, ow_hbm, gate_hbm, up_hbm, down_hbm,
    sout_ref, normed_ref,
    ow_v, gate_v, up_v, down_v, proj, projr, outg, full, part, partr, res, ret, sq,
    w_sem, p_send, p_recv, d_send, d_recv, f_send, f_recv, s_send, s_recv, r_send, r_recv,
    q_send, q_recv,
):
    me = lax.axis_index("ep")
    hid = lax.axis_index("hid")
    loc = lax.rem(me, EXPERTS)
    base = me - loc
    tok, quarter = stream_ref.shape
    rows = EXPERTS * MOST
    shifts = EXPERTS // CHUNKS
    crows = rows // CHUNKS

    def ahead(i):
        return base + lax.rem(loc + i, EXPERTS)

    def behind(i):
        return base + lax.rem(loc + EXPERTS - i, EXPERTS)

    def hid_up(j):
        return lax.rem(hid + j, HID)

    def cols(j):
        return pl.ds(pl.multiple_of(hid_up(j) * quarter, quarter), quarter)

    def slot(i):
        return pl.ds(pl.multiple_of(i * MOST, MOST), MOST)

    def chunk(c):
        return pl.ds(c * crows, crows)

    loads = [
        pltpu.make_async_copy(src, dst, w_sem.at[n])
        for n, (src, dst) in enumerate(
            [(ow_hbm, ow_v), (gate_hbm, gate_v), (up_hbm, up_v), (down_hbm, down_v)]
        )
    ]
    for load in loads:
        load.start()

    barrier = pltpu.get_barrier_semaphore()

    def greet(i, carry):
        pl.semaphore_signal(
            barrier, inc=1, device_id={"ep": ahead(i), "hid": hid},
            device_id_type=pl.DeviceIdType.MESH,
        )
        return carry

    lax.fori_loop(1, EXPERTS, greet, 0)
    for j in range(1, HID):
        pl.semaphore_signal(
            barrier, inc=1, device_id={"ep": me, "hid": hid_up(j)},
            device_id_type=pl.DeviceIdType.MESH,
        )

    def over_hid(src, dst, send, recv, j):
        return pltpu.make_async_remote_copy(
            src_ref=src, dst_ref=dst, send_sem=send, recv_sem=recv,
            device_id={"ep": me, "hid": hid_up(j)}, device_id_type=pl.DeviceIdType.MESH,
        )

    def p_copy(j):
        return over_hid(proj.at[j], projr.at[j], p_send.at[j], p_recv.at[j], j)

    def f_copy(j, c):
        return pltpu.make_async_remote_copy(
            src_ref=full.at[0, chunk(c)], dst_ref=full.at[j, chunk(c)],
            send_sem=f_send.at[j, c], recv_sem=f_recv.at[j, c],
            device_id={"ep": me, "hid": hid_up(HID - j)}, device_id_type=pl.DeviceIdType.MESH,
        )

    def s_copy(j, c):
        return over_hid(
            part.at[j, chunk(c)], partr.at[j, chunk(c)], s_send.at[j, c], s_recv.at[j, c], j
        )

    def q_copy(j):
        return over_hid(sq.at[0], sq.at[j], q_send.at[j], q_recv.at[j], j)

    def d_copy(i):
        return pltpu.make_async_remote_copy(
            src_ref=outg.at[slot(i)], dst_ref=full.at[0, slot(i)],
            send_sem=d_send.at[i], recv_sem=d_recv.at[i],
            device_id={"ep": ahead(i), "hid": hid}, device_id_type=pl.DeviceIdType.MESH,
        )

    def r_copy(i):
        return pltpu.make_async_remote_copy(
            src_ref=res.at[slot(i)], dst_ref=ret.at[slot(i)],
            send_sem=r_send.at[i], recv_sem=r_recv.at[i],
            device_id={"ep": behind(i), "hid": hid}, device_id_type=pl.DeviceIdType.MESH,
        )

    def each(low, high, act):
        def body(i, carry):
            act(i)
            return carry

        lax.fori_loop(low, high, body, 0)

    def span(c):
        return max(1, c * shifts), (c + 1) * shifts

    att = att_ref[...]
    loads[0].wait()
    for j in range(HID):
        proj[j] = dot(att, ow_v[:, cols(j)]).astype(BF)
    pl.semaphore_wait(barrier, EXPERTS - 1 + HID - 1)
    for j in (2, 1, 3):
        p_copy(j).start()

    column = lax.broadcasted_iota(jnp.int32, (tok, rows), 1)
    expert = (loc + column // MOST) % EXPERTS
    place = (column % MOST).astype(F32)
    named = jnp.zeros((tok, rows), F32)
    weight = jnp.zeros((tok, rows), F32)
    for k in range(routes_ref.shape[1]):
        same = routes_ref[:, k : k + 1] == expert
        named = named + jnp.where(same, 1.0, 0.0)
        weight = weight + jnp.where(same, rw_ref[:, k : k + 1], 0.0)
    earlier = jnp.where(
        lax.broadcasted_iota(jnp.int32, (tok, tok), 1)
        < lax.broadcasted_iota(jnp.int32, (tok, tok), 0),
        1.0,
        0.0,
    ).astype(BF)
    rank = dot(earlier, named.astype(BF))
    hit = jnp.where(rank == place, named, 0.0)
    pick = hit.astype(BF).T
    scaled = hit * weight
    high = scaled.astype(BF)
    low = (scaled - high.astype(F32)).astype(BF)

    total = proj[0].astype(F32)
    for j in range(1, HID):
        p_copy(j).wait_recv()
        total = total + projr[j].astype(F32)
    mixed = (stream_ref[...].astype(F32) + total.astype(BF).astype(F32)).astype(BF)

    for c in range(CHUNKS):
        block = dot(pick[c * crows : (c + 1) * crows], mixed).astype(BF)
        outg[chunk(c)] = block
        if c == 0:
            full[0, 0:MOST] = block[0:MOST]
        each(*span(c), lambda i: d_copy(i).start())

    def gather(c):
        each(*span(c), lambda i: d_copy(i).wait_recv())
        for j in (2, 1, 3):
            f_copy(j, c).start()

    def compute(c):
        gate = jnp.zeros((crows, gate_v.shape[1]), F32)
        up = jnp.zeros((crows, gate_v.shape[1]), F32)
        for j in (0, 1, 3, 2):
            if j:
                f_copy(j, c).wait_recv()
            features = full[j, chunk(c)]
            gate = gate + dot(features, gate_v[cols(j), :])
            up = up + dot(features, up_v[cols(j), :])
        hidden = (jnp.maximum(gate, 0.0) * up).astype(BF)
        for j in (2, 1, 3, 0):
            part[j, chunk(c)] = dot(hidden, down_v[:, cols(j)]).astype(BF)
            if j:
                s_copy(j, c).start()

    def give_back(c):
        value = part[0, chunk(c)].astype(F32)
        for j in range(1, HID):
            s_copy(j, c).wait_recv()
            value = value + partr[j, chunk(c)].astype(F32)
        value = value.astype(BF)
        res[chunk(c)] = value
        if c == 0:
            ret[0:MOST] = value[0:MOST]
        each(*span(c), lambda i: r_copy(i).start())

    gather(0)
    gather(1)
    for n in range(1, 4):
        loads[n].wait()
    compute(0)
    gather(2)
    compute(1)
    gather(3)
    give_back(0)
    compute(2)
    give_back(1)
    compute(3)
    give_back(2)
    give_back(3)

    mixture = jnp.zeros((tok, quarter), F32)
    for c in range(CHUNKS):
        each(*span(c), lambda i: r_copy(i).wait_recv())
        back = ret[chunk(c)]
        mixture = mixture + dot(high[:, c * crows : (c + 1) * crows], back)
        mixture = mixture + dot(low[:, c * crows : (c + 1) * crows], back)
    residual = mixed.astype(F32) + mixture
    sout_ref[...] = residual.astype(BF)
    squares = residual * residual
    lanes = squares[:, 0:128]
    for n in range(1, quarter // 128):
        lanes = lanes + squares[:, n * 128 : (n + 1) * 128]
    sq[0] = lanes
    for j in (2, 1, 3):
        q_copy(j).start()

    for j in range(1, HID):
        p_copy(j).wait_send()
        for c in range(CHUNKS):
            f_copy(j, c).wait_send()
            s_copy(j, c).wait_send()
    each(1, EXPERTS, lambda i: d_copy(i).wait_send())
    each(1, EXPERTS, lambda i: r_copy(i).wait_send())

    for j in range(1, HID):
        q_copy(j).wait_recv()
        lanes = lanes + sq[j]
    rms = jnp.sum(lanes, axis=1, keepdims=True) / (quarter * HID)
    normed_ref[...] = (residual * lax.rsqrt(rms + EPSILON) * gain_ref[...]).astype(BF)
    for j in range(1, HID):
        q_copy(j).wait_send()


def on_device(attention, stream, o_weight, routes, route_weight, gate_up, down_proj, norm_gain):
    tok, quarter = stream.shape
    full_width = quarter * HID
    width = gate_up.shape[3]
    rows = EXPERTS * MOST
    gate = gate_up[0, :, 0, :]
    up = gate_up[0, :, 1, :]
    down = down_proj[0]
    vmem = pl.BlockSpec(memory_space=pltpu.VMEM)
    hbm = pl.BlockSpec(memory_space=pl.ANY)
    dma = pltpu.SemaphoreType.DMA
    return pl.pallas_call(
        kernel,
        out_shape=(
            jax.ShapeDtypeStruct((tok, quarter), BF),
            jax.ShapeDtypeStruct((tok, quarter), BF),
        ),
        in_specs=[vmem] * 5 + [hbm] * 4,
        out_specs=(vmem, vmem),
        scratch_shapes=[
            pltpu.VMEM(o_weight.shape, BF),
            pltpu.VMEM(gate.shape, BF),
            pltpu.VMEM(up.shape, BF),
            pltpu.VMEM(down.shape, BF),
            pltpu.VMEM((HID, tok, quarter), BF),
            pltpu.VMEM((HID, tok, quarter), BF),
            pltpu.VMEM((rows, quarter), BF),
            pltpu.VMEM((HID, rows, quarter), BF),
            pltpu.VMEM((HID, rows, quarter), BF),
            pltpu.VMEM((HID, rows, quarter), BF),
            pltpu.VMEM((rows, quarter), BF),
            pltpu.VMEM((rows, quarter), BF),
            pltpu.VMEM((HID, tok, 128), F32),
            dma((4,)),
            dma((HID,)), dma((HID,)),
            dma((EXPERTS,)), dma((EXPERTS,)),
            dma((HID, CHUNKS)), dma((HID, CHUNKS)),
            dma((HID, CHUNKS)), dma((HID, CHUNKS)),
            dma((EXPERTS,)), dma((EXPERTS,)),
            dma((HID,)), dma((HID,)),
        ],
        compiler_params=pltpu.CompilerParams(collective_id=0, has_side_effects=True),
    )(
        attention, stream, routes, route_weight, norm_gain.reshape(1, quarter),
        o_weight, gate, up, down,
    )


def solution(mesh):
    in_specs = (
        P("ep", "hid"),
        P("ep", "hid"),
        P("hid", None),
        P("ep", None),
        P("ep", None),
        P("ep", None, None, "hid"),
        P("ep", "hid", None),
        P("hid"),
    )
    out_specs = (P("ep", "hid"), P("ep", "hid"))
    return jax.shard_map(
        on_device, mesh=mesh, in_specs=in_specs, out_specs=out_specs, check_vma=False
    )
```

```python
import jax
import jax.numpy as jnp
from jax import lax
from jax.experimental import pallas as pl
from jax.experimental.pallas import tpu as pltpu
from jax.sharding import PartitionSpec as P

EXPERTS = 32
MOST = 16
HID = 4
CHUNKS = 4
EPSILON = 1e-06
BF = jnp.bfloat16
F32 = jnp.float32


def dot(a, b):
    return jnp.dot(a, b, preferred_element_type=F32)


def dot_t(a, b):
    return lax.dot_general(a, b, (((1,), (1,)), ((), ())), preferred_element_type=F32)


def kernel(
    att_ref, stream_ref, routes_ref, rw_ref, ow_hbm, gu_hbm, down_hbm,
    residual_ref, scaled_ref,
    ow_v, gu_v, down_v, proj, projr, outg, full, part, partr, passing, res, ret, sq,
    w_sem, p_send, p_recv, d_send, d_recv, f_send, f_recv, s_send, s_recv, r_send, r_recv,
    q_send, q_recv,
):
    me = lax.axis_index("ep")
    hid = lax.axis_index("hid")
    loc = lax.rem(me, EXPERTS)
    base = me - loc
    tok, quarter = stream_ref.shape
    rows = EXPERTS * MOST
    shifts = EXPERTS // CHUNKS
    crows = rows // CHUNKS
    hrows = crows // 2
    width = gu_v.shape[0] // 2

    def ahead(i):
        return base + lax.rem(loc + i, EXPERTS)

    def behind(i):
        return base + lax.rem(loc + EXPERTS - i, EXPERTS)

    def hid_up(j):
        return lax.rem(hid + j, HID)

    def cols(j):
        return pl.ds(pl.multiple_of(hid_up(j) * quarter, quarter), quarter)

    def slot(i):
        return pl.ds(pl.multiple_of(i * MOST, MOST), MOST)

    def chunk(c):
        return pl.ds(c * crows, crows)

    def half(c, b):
        return pl.ds(c * crows + b * hrows, hrows)

    loads = [
        pltpu.make_async_copy(src, dst, w_sem.at[n])
        for n, (src, dst) in enumerate(
            [(ow_hbm, ow_v), (gu_hbm, gu_v), (down_hbm, down_v)]
        )
    ]
    for load in loads:
        load.start()

    barrier = pltpu.get_barrier_semaphore()

    def greet(i, carry):
        pl.semaphore_signal(
            barrier, inc=1, device_id={"ep": ahead(i), "hid": hid},
            device_id_type=pl.DeviceIdType.MESH,
        )
        return carry

    lax.fori_loop(1, EXPERTS, greet, 0)
    for j in range(1, HID):
        pl.semaphore_signal(
            barrier, inc=1, device_id={"ep": me, "hid": hid_up(j)},
            device_id_type=pl.DeviceIdType.MESH,
        )

    def over_hid(src, dst, send, recv, j):
        return pltpu.make_async_remote_copy(
            src_ref=src, dst_ref=dst, send_sem=send, recv_sem=recv,
            device_id={"ep": me, "hid": hid_up(j)}, device_id_type=pl.DeviceIdType.MESH,
        )

    def p_copy(j):
        return over_hid(proj.at[j], projr.at[j], p_send.at[j], p_recv.at[j], j)

    def f_copy(j, c):
        return pltpu.make_async_remote_copy(
            src_ref=full.at[0, chunk(c)], dst_ref=full.at[j, chunk(c)],
            send_sem=f_send.at[j, c], recv_sem=f_recv.at[j, c],
            device_id={"ep": me, "hid": hid_up(HID - j)}, device_id_type=pl.DeviceIdType.MESH,
        )

    def f_pass(b, c):
        j = 1 + 2 * b
        return pltpu.make_async_remote_copy(
            src_ref=full.at[j, half(c, b)], dst_ref=full.at[2, half(c, b)],
            send_sem=f_send.at[2 * b, c], recv_sem=f_recv.at[2 * b, c],
            device_id={"ep": me, "hid": hid_up(HID - j)}, device_id_type=pl.DeviceIdType.MESH,
        )

    def s_copy(j, b, c):
        return over_hid(
            part.at[j, half(c, b)], partr.at[j // 2, half(c, b)],
            s_send.at[j // 2, b, c], s_recv.at[j // 2, b, c], j
        )

    def s_pass(b, c):
        return over_hid(
            part.at[2, half(c, b)], passing.at[half(c, b)],
            s_send.at[2, b, c], s_recv.at[2, b, c], 1 + 2 * b
        )

    def q_copy(j):
        return over_hid(sq.at[0], sq.at[j], q_send.at[j], q_recv.at[j], j)

    def d_copy(i):
        return pltpu.make_async_remote_copy(
            src_ref=outg.at[slot(i)], dst_ref=full.at[0, slot(i)],
            send_sem=d_send.at[i], recv_sem=d_recv.at[i],
            device_id={"ep": ahead(i), "hid": hid}, device_id_type=pl.DeviceIdType.MESH,
        )

    def r_copy(i):
        return pltpu.make_async_remote_copy(
            src_ref=res.at[slot(i)], dst_ref=ret.at[slot(i)],
            send_sem=r_send.at[i], recv_sem=r_recv.at[i],
            device_id={"ep": behind(i), "hid": hid}, device_id_type=pl.DeviceIdType.MESH,
        )

    def each(low, high, act):
        def body(i, carry):
            act(i)
            return carry

        lax.fori_loop(low, high, body, 0)

    def span(c):
        return max(1, c * shifts), (c + 1) * shifts

    att = att_ref[...]
    loads[0].wait()
    for j in range(HID):
        proj[j] = dot(att, ow_v[:, cols(j)]).astype(BF)
    pl.semaphore_wait(barrier, EXPERTS - 1 + HID - 1)
    for j in (2, 1, 3):
        p_copy(j).start()

    row = lax.broadcasted_iota(jnp.int32, (rows, tok), 0)
    expert = (loc + row // MOST) % EXPERTS
    place = (row % MOST).astype(F32)
    named = jnp.zeros((rows, tok), F32)
    weight = jnp.zeros((rows, tok), F32)
    for k in range(routes_ref.shape[0]):
        same = routes_ref[k : k + 1, :] == expert
        named = named + jnp.where(same, 1.0, 0.0)
        weight = weight + jnp.where(same, rw_ref[k : k + 1, :], 0.0)
    earlier = jnp.where(
        lax.broadcasted_iota(jnp.int32, (tok, tok), 0)
        < lax.broadcasted_iota(jnp.int32, (tok, tok), 1),
        1.0,
        0.0,
    ).astype(BF)
    rank = dot(named.astype(BF), earlier)
    hit = jnp.where(rank == place, named, 0.0)
    pick = hit.astype(BF)
    scaled = (hit * weight).T
    high = scaled.astype(BF)
    low = (scaled - high.astype(F32)).astype(BF)

    total = proj[0].astype(F32)
    for j in range(1, HID):
        p_copy(j).wait_recv()
        total = total + projr[j].astype(F32)
    mixed = (stream_ref[...].astype(F32) + total.astype(BF).astype(F32)).astype(BF)

    for c in range(CHUNKS):
        block = dot(pick[c * crows : (c + 1) * crows], mixed).astype(BF)
        outg[chunk(c)] = block
        if c == 0:
            full[0, 0:MOST] = block[0:MOST]
        each(*span(c), lambda i: d_copy(i).start())

    def gather(c):
        each(*span(c), lambda i: d_copy(i).wait_recv())
        for j in (1, 3):
            f_copy(j, c).start()

    def gather_on(c):
        for b in range(2):
            f_copy(1 + 2 * b, c).wait_recv()
            f_pass(b, c).start()

    def compute(c):
        gate = jnp.zeros((crows, width), F32)
        up = jnp.zeros((crows, width), F32)
        for j in (0, 1, 3, 2):
            if j == 2:
                f_pass(0, c).wait_recv()
                f_pass(1, c).wait_recv()
            features = full[j, chunk(c)]
            gate = gate + dot_t(features, gu_v[:width, cols(j)])
            up = up + dot_t(features, gu_v[width:, cols(j)])
        hidden = (jnp.maximum(gate, 0.0) * up).astype(BF)
        part[2, chunk(c)] = dot(hidden, down_v[:, cols(2)]).astype(BF)
        for b in range(2):
            s_pass(b, c).start()
        for j in (1, 3):
            part[j, chunk(c)] = dot(hidden, down_v[:, cols(j)]).astype(BF)
            s_copy(j, (3 - j) // 2, c).start()
        part[0, chunk(c)] = dot(hidden, down_v[:, cols(0)]).astype(BF)

    def sum_on(c):
        for b in range(2):
            j = 1 + 2 * b
            s_pass(b, c).wait_recv()
            both = part[j, half(c, b)].astype(F32) + passing[half(c, b)].astype(F32)
            part[j, half(c, b)] = both.astype(BF)
            s_copy(j, b, c).start()

    def give_back(c):
        for j in (1, 3):
            for b in range(2):
                s_copy(j, b, c).wait_recv()
        value = part[0, chunk(c)].astype(F32) + partr[0, chunk(c)].astype(F32)
        value = (value + partr[1, chunk(c)].astype(F32)).astype(BF)
        res[chunk(c)] = value
        if c == 0:
            ret[0:MOST] = value[0:MOST]
        each(*span(c), lambda i: r_copy(i).start())

    gather(0)
    gather(1)
    gather_on(0)
    for n in range(1, 3):
        loads[n].wait()
    gather(2)
    gather_on(1)
    compute(0)
    gather(3)
    gather_on(2)
    compute(1)
    gather_on(3)
    sum_on(0)
    compute(2)
    sum_on(1)
    give_back(0)
    compute(3)
    sum_on(2)
    give_back(1)
    sum_on(3)
    give_back(2)
    give_back(3)

    mixture = jnp.zeros((tok, quarter), F32)
    for c in range(CHUNKS):
        each(*span(c), lambda i: r_copy(i).wait_recv())
        back = ret[chunk(c)]
        mixture = mixture + dot(high[:, c * crows : (c + 1) * crows], back)
        mixture = mixture + dot(low[:, c * crows : (c + 1) * crows], back)
    residual = mixed.astype(F32) + mixture
    residual_ref[...] = residual
    squares = residual * residual
    lanes = squares[:, 0:128]
    for n in range(1, quarter // 128):
        lanes = lanes + squares[:, n * 128 : (n + 1) * 128]
    sq[0] = lanes
    for j in (2, 1, 3):
        q_copy(j).start()

    for j in range(1, HID):
        p_copy(j).wait_send()
    for c in range(CHUNKS):
        for b in range(2):
            f_copy(1 + 2 * b, c).wait_send()
            f_pass(b, c).wait_send()
            s_pass(b, c).wait_send()
            s_copy(1, b, c).wait_send()
            s_copy(3, b, c).wait_send()
    each(1, EXPERTS, lambda i: d_copy(i).wait_send())
    each(1, EXPERTS, lambda i: r_copy(i).wait_send())

    for j in range(1, HID):
        q_copy(j).wait_recv()
        lanes = lanes + sq[j]
    rms = jnp.sum(lanes, axis=1, keepdims=True) / (quarter * HID)
    scaled_ref[...] = residual * lax.rsqrt(rms + EPSILON)
    for j in range(1, HID):
        q_copy(j).wait_send()


def on_device(attention, stream, o_weight, routes, route_weight, gate_up, down_proj, norm_gain):
    tok, quarter = stream.shape
    full_width = quarter * HID
    width = gate_up.shape[3]
    rows = EXPERTS * MOST
    gate_up_t = gate_up[0].transpose(1, 2, 0).reshape(2 * width, full_width)
    down = down_proj[0]
    vmem = pl.BlockSpec(memory_space=pltpu.VMEM)
    hbm = pl.BlockSpec(memory_space=pl.ANY)
    dma = pltpu.SemaphoreType.DMA
    residual, scaled = pl.pallas_call(
        kernel,
        out_shape=(
            jax.ShapeDtypeStruct((tok, quarter), F32),
            jax.ShapeDtypeStruct((tok, quarter), F32),
        ),
        in_specs=[vmem] * 4 + [hbm] * 3,
        out_specs=(vmem, vmem),
        scratch_shapes=[
            pltpu.VMEM(o_weight.shape, BF),
            pltpu.VMEM(gate_up_t.shape, BF),
            pltpu.VMEM(down.shape, BF),
            pltpu.VMEM((HID, tok, quarter), BF),
            pltpu.VMEM((HID, tok, quarter), BF),
            pltpu.VMEM((rows, quarter), BF),
            pltpu.VMEM((HID, rows, quarter), BF),
            pltpu.VMEM((HID, rows, quarter), BF),
            pltpu.VMEM((2, rows, quarter), BF),
            pltpu.VMEM((rows, quarter), BF),
            pltpu.VMEM((rows, quarter), BF),
            pltpu.VMEM((rows, quarter), BF),
            pltpu.VMEM((HID, tok, 128), F32),
            dma((3,)),
            dma((HID,)), dma((HID,)),
            dma((EXPERTS,)), dma((EXPERTS,)),
            dma((HID, CHUNKS)), dma((HID, CHUNKS)),
            dma((3, 2, CHUNKS)), dma((3, 2, CHUNKS)),
            dma((EXPERTS,)), dma((EXPERTS,)),
            dma((HID,)), dma((HID,)),
        ],
        compiler_params=pltpu.CompilerParams(collective_id=0, has_side_effects=True),
    )(attention, stream, routes.T, route_weight.T, o_weight, gate_up_t, down)
    normed = (scaled * norm_gain[None, :]).astype(BF)
    return residual.astype(BF), normed


def solution(mesh):
    in_specs = (
        P("ep", "hid"),
        P("ep", "hid"),
        P("hid", None),
        P("ep", None),
        P("ep", None),
        P("ep", None, None, "hid"),
        P("ep", "hid", None),
        P("hid"),
    )
    out_specs = (P("ep", "hid"), P("ep", "hid"))
    return jax.shard_map(
        on_device, mesh=mesh, in_specs=in_specs, out_specs=out_specs, check_vma=False
    )
```

```python
import jax
import jax.numpy as jnp
from jax import lax
from jax.experimental import pallas as pl
from jax.experimental.pallas import tpu as pltpu
from jax.sharding import PartitionSpec as P

EXPERTS = 32
MOST = 16
HID = 4
CHUNKS = 4
EPSILON = 1e-06
BF = jnp.bfloat16
F32 = jnp.float32


def dot(a, b):
    return jnp.dot(a, b, preferred_element_type=F32)


def dot_t(a, b):
    return lax.dot_general(a, b, (((1,), (1,)), ((), ())), preferred_element_type=F32)


def kernel(
    att_ref, stream_ref, routes_ref, rw_ref, ow_hbm, gu_hbm, down_hbm,
    residual_ref, inverse_ref,
    ow_v, gu_v, down_v, proj, projr, outg, full, part, partr, passing, res, ret, sq,
    w_sem, p_send, p_recv, d_send, d_recv, f_send, f_recv, s_send, s_recv, r_send, r_recv,
    q_send, q_recv,
):
    me = lax.axis_index("ep")
    hid = lax.axis_index("hid")
    loc = lax.rem(me, EXPERTS)
    base = me - loc
    tok, quarter = stream_ref.shape
    rows = EXPERTS * MOST
    crows = rows // CHUNKS
    hrows = crows // 2
    width = gu_v.shape[0] // 2

    core, zed, why = lax.rem(loc, 2), lax.rem(loc // 2, 8), loc // 16

    def distance(c, b):
        near = (1, 0, 3, 2)[c]
        return near if b == 0 else (4 if c == 1 else 8 - near)

    def ahead(c, b, q):
        return (
            base + 16 * lax.rem(why + q // 2, 2) + 2 * lax.rem(zed + distance(c, b), 8)
            + lax.rem(core + q % 2, 2)
        )

    def behind(c, b, q):
        return (
            base + 16 * lax.rem(why + q // 2, 2) + 2 * lax.rem(zed + 8 - distance(c, b), 8)
            + lax.rem(core + q % 2, 2)
        )

    def hid_up(j):
        return lax.rem(hid + j, HID)

    def cols(j):
        return pl.ds(pl.multiple_of(hid_up(j) * quarter, quarter), quarter)

    def slot(i):
        return pl.ds(pl.multiple_of(i * MOST, MOST), MOST)

    def chunk(c):
        return pl.ds(c * crows, crows)

    def half(c, b):
        return pl.ds(c * crows + b * hrows, hrows)

    loads = [
        pltpu.make_async_copy(src, dst, w_sem.at[n])
        for n, (src, dst) in enumerate(
            [(ow_hbm, ow_v), (gu_hbm, gu_v), (down_hbm, down_v)]
        )
    ]
    for load in loads:
        load.start()

    barrier = pltpu.get_barrier_semaphore()

    def greet(i, carry):
        pl.semaphore_signal(
            barrier, inc=1, device_id={"ep": base + lax.rem(loc + i, EXPERTS), "hid": hid},
            device_id_type=pl.DeviceIdType.MESH,
        )
        return carry

    lax.fori_loop(1, EXPERTS, greet, 0)
    for j in range(1, HID):
        pl.semaphore_signal(
            barrier, inc=1, device_id={"ep": me, "hid": hid_up(j)},
            device_id_type=pl.DeviceIdType.MESH,
        )

    def over_hid(src, dst, send, recv, j):
        return pltpu.make_async_remote_copy(
            src_ref=src, dst_ref=dst, send_sem=send, recv_sem=recv,
            device_id={"ep": me, "hid": hid_up(j)}, device_id_type=pl.DeviceIdType.MESH,
        )

    def p_copy(j):
        return over_hid(proj.at[j], projr.at[j], p_send.at[j], p_recv.at[j], j)

    def f_copy(j, c):
        return pltpu.make_async_remote_copy(
            src_ref=full.at[0, chunk(c)], dst_ref=full.at[j, chunk(c)],
            send_sem=f_send.at[j, c], recv_sem=f_recv.at[j, c],
            device_id={"ep": me, "hid": hid_up(HID - j)}, device_id_type=pl.DeviceIdType.MESH,
        )

    def f_pass(b, c):
        j = 1 + 2 * b
        return pltpu.make_async_remote_copy(
            src_ref=full.at[j, half(c, b)], dst_ref=full.at[2, half(c, b)],
            send_sem=f_send.at[2 * b, c], recv_sem=f_recv.at[2 * b, c],
            device_id={"ep": me, "hid": hid_up(HID - j)}, device_id_type=pl.DeviceIdType.MESH,
        )

    def s_copy(j, b, c):
        return over_hid(
            part.at[j, half(c, b)], partr.at[j // 2, half(c, b)],
            s_send.at[j // 2, b, c], s_recv.at[j // 2, b, c], j
        )

    def s_pass(b, c):
        return over_hid(
            part.at[2, half(c, b)], passing.at[half(c, b)],
            s_send.at[2, b, c], s_recv.at[2, b, c], 1 + 2 * b
        )

    def q_copy(j):
        return over_hid(sq.at[0], sq.at[j], q_send.at[j], q_recv.at[j], j)

    def d_copy(c, b, q):
        n = c * 8 + b * 4 + q
        return pltpu.make_async_remote_copy(
            src_ref=outg.at[slot(n)], dst_ref=full.at[0, slot(n)],
            send_sem=d_send.at[n], recv_sem=d_recv.at[n],
            device_id={"ep": ahead(c, b, q), "hid": hid}, device_id_type=pl.DeviceIdType.MESH,
        )

    def r_copy(c, b, q):
        n = c * 8 + b * 4 + q
        return pltpu.make_async_remote_copy(
            src_ref=res.at[slot(n)], dst_ref=ret.at[slot(n)],
            send_sem=r_send.at[n], recv_sem=r_recv.at[n],
            device_id={"ep": behind(c, b, q), "hid": hid}, device_id_type=pl.DeviceIdType.MESH,
        )

    def each(c, act):
        def both(q, carry):
            act(c, 0, q)
            act(c, 1, q)
            return carry

        if c == 1:
            act(c, 1, 0)
        lax.fori_loop(1 if c == 1 else 0, 4, both, 0)

    own = pl.ds(crows, MOST)

    att = att_ref[...]
    loads[0].wait()
    for j in range(HID):
        proj[j] = dot(att, ow_v[:, cols(j)]).astype(BF)
    pl.semaphore_wait(barrier, EXPERTS - 1 + HID - 1)
    for j in (2, 1, 3):
        p_copy(j).start()

    row = lax.broadcasted_iota(jnp.int32, (rows, tok), 0)
    number = row // MOST
    near = (number // 8) ^ 1
    far = jnp.where(number // 8 == 1, 4, 8 - near)
    step = jnp.where((number // 4) % 2 == 0, near, far)
    expert = (
        16 * ((why + (number % 4) // 2) % 2) + 2 * ((zed + step) % 8) + (core + number) % 2
    )
    place = (row % MOST).astype(F32)
    named = jnp.zeros((rows, tok), F32)
    weight = jnp.zeros((rows, tok), F32)
    for k in range(routes_ref.shape[0]):
        same = routes_ref[k : k + 1, :] == expert
        named = named + jnp.where(same, 1.0, 0.0)
        weight = weight + jnp.where(same, rw_ref[k : k + 1, :], 0.0)
    earlier = jnp.where(
        lax.broadcasted_iota(jnp.int32, (tok, tok), 0)
        < lax.broadcasted_iota(jnp.int32, (tok, tok), 1),
        1.0,
        0.0,
    ).astype(BF)
    rank = dot(named.astype(BF), earlier)
    hit = jnp.where(rank == place, named, 0.0)
    pick = hit.astype(BF)
    scaled = (hit * weight).T
    high = scaled.astype(BF)
    low = (scaled - high.astype(F32)).astype(BF)

    total = proj[0].astype(F32)
    for j in range(1, HID):
        p_copy(j).wait_recv()
        total = total + projr[j].astype(F32)
    mixed = (stream_ref[...].astype(F32) + total.astype(BF).astype(F32)).astype(BF)

    for c in range(CHUNKS):
        block = dot(pick[c * crows : (c + 1) * crows], mixed).astype(BF)
        outg[chunk(c)] = block
        if c == 1:
            full[0, own] = block[0:MOST]
        each(c, lambda *n: d_copy(*n).start())

    def gather(c):
        each(c, lambda *n: d_copy(*n).wait_recv())
        for j in (1, 3):
            f_copy(j, c).start()

    def gather_on(c):
        for b in range(2):
            f_copy(1 + 2 * b, c).wait_recv()
            f_pass(b, c).start()

    def compute(c):
        gate = jnp.zeros((crows, width), F32)
        up = jnp.zeros((crows, width), F32)
        for j in (0, 1, 3, 2):
            if j == 2:
                f_pass(0, c).wait_recv()
                f_pass(1, c).wait_recv()
            features = full[j, chunk(c)]
            gate = gate + dot_t(features, gu_v[:width, cols(j)])
            up = up + dot_t(features, gu_v[width:, cols(j)])
        hidden = (jnp.maximum(gate, 0.0) * up).astype(BF)
        part[2, chunk(c)] = dot(hidden, down_v[:, cols(2)]).astype(BF)
        for b in range(2):
            s_pass(b, c).start()
        for j in (1, 3):
            part[j, chunk(c)] = dot(hidden, down_v[:, cols(j)]).astype(BF)
            s_copy(j, (3 - j) // 2, c).start()
        part[0, chunk(c)] = dot(hidden, down_v[:, cols(0)]).astype(BF)

    def sum_on(c):
        for b in range(2):
            j = 1 + 2 * b
            s_pass(b, c).wait_recv()
            both = part[j, half(c, b)].astype(F32) + passing[half(c, b)].astype(F32)
            part[j, half(c, b)] = both.astype(BF)
            s_copy(j, b, c).start()

    def give_back(c):
        for j in (1, 3):
            for b in range(2):
                s_copy(j, b, c).wait_recv()
        value = part[0, chunk(c)].astype(F32) + partr[0, chunk(c)].astype(F32)
        value = (value + partr[1, chunk(c)].astype(F32)).astype(BF)
        res[chunk(c)] = value
        if c == 1:
            ret[own] = value[0:MOST]
        each(c, lambda *n: r_copy(*n).start())

    gather(0)
    for n in range(1, 3):
        loads[n].wait()
    gather_on(0)
    gather(1)
    compute(0)
    gather_on(1)
    gather(2)
    sum_on(0)
    compute(1)
    gather_on(2)
    gather(3)
    give_back(0)
    sum_on(1)
    compute(2)
    gather_on(3)
    give_back(1)
    sum_on(2)
    compute(3)
    give_back(2)
    sum_on(3)
    give_back(3)

    mixture = jnp.zeros((tok, quarter), F32)
    for c in range(CHUNKS):
        each(c, lambda *n: r_copy(*n).wait_recv())
        back = ret[chunk(c)]
        mixture = mixture + dot(high[:, c * crows : (c + 1) * crows], back)
        mixture = mixture + dot(low[:, c * crows : (c + 1) * crows], back)
    residual = mixed.astype(F32) + mixture
    residual_ref[...] = residual
    squares = residual * residual
    lanes = squares[:, 0:128]
    for n in range(1, quarter // 128):
        lanes = lanes + squares[:, n * 128 : (n + 1) * 128]
    sq[0] = lanes
    for j in (2, 1, 3):
        q_copy(j).start()

    for j in range(1, HID):
        p_copy(j).wait_send()
    for c in range(CHUNKS):
        for b in range(2):
            f_copy(1 + 2 * b, c).wait_send()
            f_pass(b, c).wait_send()
            s_pass(b, c).wait_send()
            s_copy(1, b, c).wait_send()
            s_copy(3, b, c).wait_send()
    for c in range(CHUNKS):
        each(c, lambda *n: d_copy(*n).wait_send())
        each(c, lambda *n: r_copy(*n).wait_send())

    for j in range(1, HID):
        q_copy(j).wait_recv()
        lanes = lanes + sq[j]
    rms = jnp.sum(lanes, axis=1, keepdims=True) / (quarter * HID)
    inverse_ref[...] = jnp.broadcast_to(lax.rsqrt(rms + EPSILON), residual.shape)
    for j in range(1, HID):
        q_copy(j).wait_send()


def on_device(attention, stream, o_weight, routes, route_weight, gate_up, down_proj, norm_gain):
    tok, quarter = stream.shape
    full_width = quarter * HID
    width = gate_up.shape[3]
    rows = EXPERTS * MOST
    gate_up_t = gate_up[0].transpose(1, 2, 0).reshape(2 * width, full_width)
    down = down_proj[0]
    vmem = pl.BlockSpec(memory_space=pltpu.VMEM)
    hbm = pl.BlockSpec(memory_space=pl.ANY)
    dma = pltpu.SemaphoreType.DMA
    residual, inverse = pl.pallas_call(
        kernel,
        out_shape=(
            jax.ShapeDtypeStruct((tok, quarter), F32),
            jax.ShapeDtypeStruct((tok, quarter), F32),
        ),
        in_specs=[vmem] * 4 + [hbm] * 3,
        out_specs=(vmem, vmem),
        scratch_shapes=[
            pltpu.VMEM(o_weight.shape, BF),
            pltpu.VMEM(gate_up_t.shape, BF),
            pltpu.VMEM(down.shape, BF),
            pltpu.VMEM((HID, tok, quarter), BF),
            pltpu.VMEM((HID, tok, quarter), BF),
            pltpu.VMEM((rows, quarter), BF),
            pltpu.VMEM((HID, rows, quarter), BF),
            pltpu.VMEM((HID, rows, quarter), BF),
            pltpu.VMEM((2, rows, quarter), BF),
            pltpu.VMEM((rows, quarter), BF),
            pltpu.VMEM((rows, quarter), BF),
            pltpu.VMEM((rows, quarter), BF),
            pltpu.VMEM((HID, tok, 128), F32),
            dma((3,)),
            dma((HID,)), dma((HID,)),
            dma((EXPERTS,)), dma((EXPERTS,)),
            dma((HID, CHUNKS)), dma((HID, CHUNKS)),
            dma((3, 2, CHUNKS)), dma((3, 2, CHUNKS)),
            dma((EXPERTS,)), dma((EXPERTS,)),
            dma((HID,)), dma((HID,)),
        ],
        compiler_params=pltpu.CompilerParams(collective_id=0, has_side_effects=True),
    )(attention, stream, routes.T, route_weight.T, o_weight, gate_up_t, down)
    normed = (residual * inverse * norm_gain[None, :]).astype(BF)
    return residual.astype(BF), normed


def solution(mesh):
    in_specs = (
        P("ep", "hid"),
        P("ep", "hid"),
        P("hid", None),
        P("ep", None),
        P("ep", None),
        P("ep", None, None, "hid"),
        P("ep", "hid", None),
        P("hid"),
    )
    out_specs = (P("ep", "hid"), P("ep", "hid"))
    return jax.shard_map(
        on_device, mesh=mesh, in_specs=in_specs, out_specs=out_specs, check_vma=False
    )
```

```python
import jax
import jax.numpy as jnp
from jax import lax
from jax.experimental import pallas as pl
from jax.experimental.pallas import tpu as pltpu
from jax.sharding import PartitionSpec as P

EXPERTS = 32
MOST = 16
HID = 4
CHUNKS = 4
EPSILON = 1e-06
BF = jnp.bfloat16
F32 = jnp.float32


def dot(a, b):
    return jnp.dot(a, b, preferred_element_type=F32)


def dot_t(a, b):
    return lax.dot_general(a, b, (((1,), (1,)), ((), ())), preferred_element_type=F32)


def kernel(
    att_ref, stream_ref, routes_ref, rw_ref, ow_hbm, gu_hbm, down_hbm,
    residual_ref, inverse_ref,
    ow_v, gu_v, down_v, proj, projr, outg, full, part, partr, passing, res, ret, sq,
    w_sem, p_send, p_recv, d_send, d_recv, f_send, f_recv, s_send, s_recv, r_send, r_recv,
    q_send, q_recv,
):
    me = lax.axis_index("ep")
    hid = lax.axis_index("hid")
    loc = lax.rem(me, EXPERTS)
    base = me - loc
    tok, quarter = stream_ref.shape
    rows = EXPERTS * MOST
    crows = rows // CHUNKS
    hrows = crows // 2
    width = gu_v.shape[0] // 2

    core, zed, why = lax.rem(loc, 2), lax.rem(loc // 2, 8), loc // 16

    def distance(c, b):
        near = (1, 0, 3, 2)[c]
        return near if b == 0 else (4 if c == 1 else 8 - near)

    def ahead(c, b, q):
        return (
            base + 16 * lax.rem(why + q // 2, 2) + 2 * lax.rem(zed + distance(c, b), 8)
            + lax.rem(core + q % 2, 2)
        )

    def behind(c, b, q):
        return (
            base + 16 * lax.rem(why + q // 2, 2) + 2 * lax.rem(zed + 8 - distance(c, b), 8)
            + lax.rem(core + q % 2, 2)
        )

    def hid_up(j):
        return lax.rem(hid + j, HID)

    def cols(j):
        return pl.ds(pl.multiple_of(hid_up(j) * quarter, quarter), quarter)

    def slot(i):
        return pl.ds(i * MOST, MOST)

    def chunk(c):
        return pl.ds(c * crows, crows)

    def half(c, b):
        return pl.ds(c * crows + b * hrows, hrows)

    loads = [
        pltpu.make_async_copy(src, dst, w_sem.at[n])
        for n, (src, dst) in enumerate(
            [(ow_hbm, ow_v), (gu_hbm, gu_v), (down_hbm, down_v)]
        )
    ]
    for load in loads:
        load.start()

    barrier = pltpu.get_barrier_semaphore()

    def greet(i, carry):
        pl.semaphore_signal(
            barrier, inc=1, device_id={"ep": base + lax.rem(loc + i, EXPERTS), "hid": hid},
            device_id_type=pl.DeviceIdType.MESH,
        )
        return carry

    lax.fori_loop(1, EXPERTS, greet, 0)
    for j in range(1, HID):
        pl.semaphore_signal(
            barrier, inc=1, device_id={"ep": me, "hid": hid_up(j)},
            device_id_type=pl.DeviceIdType.MESH,
        )

    def over_hid(src, dst, send, recv, j):
        return pltpu.make_async_remote_copy(
            src_ref=src, dst_ref=dst, send_sem=send, recv_sem=recv,
            device_id={"ep": me, "hid": hid_up(j)}, device_id_type=pl.DeviceIdType.MESH,
        )

    def p_copy(j):
        return over_hid(proj.at[j], projr.at[j], p_send.at[j], p_recv.at[j], j)

    def f_copy(j, c):
        return pltpu.make_async_remote_copy(
            src_ref=full.at[0, chunk(c)], dst_ref=full.at[j, chunk(c)],
            send_sem=f_send.at[j, c], recv_sem=f_recv.at[j, c],
            device_id={"ep": me, "hid": hid_up(HID - j)}, device_id_type=pl.DeviceIdType.MESH,
        )

    def f_pass(b, c):
        j = 1 + 2 * b
        return pltpu.make_async_remote_copy(
            src_ref=full.at[j, half(c, b)], dst_ref=full.at[2, half(c, b)],
            send_sem=f_send.at[2 * b, c], recv_sem=f_recv.at[2 * b, c],
            device_id={"ep": me, "hid": hid_up(HID - j)}, device_id_type=pl.DeviceIdType.MESH,
        )

    def s_copy(j, b, c):
        return over_hid(
            part.at[j, half(c, b)], partr.at[j // 2, half(c, b)],
            s_send.at[j // 2, b, c], s_recv.at[j // 2, b, c], j
        )

    def s_pass(b, c):
        return over_hid(
            part.at[2, half(c, b)], passing.at[half(c, b)],
            s_send.at[2, b, c], s_recv.at[2, b, c], 1 + 2 * b
        )

    def q_copy(j):
        return over_hid(sq.at[0], sq.at[j], q_send.at[j], q_recv.at[j], j)

    def d_copy(c, b, q):
        n = c * 8 + b * 4 + q
        return pltpu.make_async_remote_copy(
            src_ref=outg.at[slot(n)], dst_ref=full.at[0, slot(n)],
            send_sem=d_send.at[c], recv_sem=d_recv.at[c],
            device_id={"ep": ahead(c, b, q), "hid": hid}, device_id_type=pl.DeviceIdType.MESH,
        )

    def r_copy(c, b, q):
        n = c * 8 + b * 4 + q
        return pltpu.make_async_remote_copy(
            src_ref=res.at[slot(n)], dst_ref=ret.at[slot(n)],
            send_sem=r_send.at[c], recv_sem=r_recv.at[c],
            device_id={"ep": behind(c, b, q), "hid": hid}, device_id_type=pl.DeviceIdType.MESH,
        )

    def each(c, act):
        for q in range(4):
            for b in range(2):
                if (c, b, q) != (1, 0, 0):
                    act(c, b, q)

    own = pl.ds(crows, MOST)

    def d_all(c):
        part_rows = pl.ds(c * crows, crows - MOST if c == 1 else crows)
        return pltpu.make_async_remote_copy(
            src_ref=outg.at[part_rows], dst_ref=full.at[0, part_rows],
            send_sem=d_send.at[c], recv_sem=d_recv.at[c],
            device_id={"ep": ahead(c, 1, 0), "hid": hid}, device_id_type=pl.DeviceIdType.MESH,
        )

    def r_all(c):
        part_rows = pl.ds(c * crows, crows - MOST if c == 1 else crows)
        return pltpu.make_async_remote_copy(
            src_ref=res.at[part_rows], dst_ref=ret.at[part_rows],
            send_sem=r_send.at[c], recv_sem=r_recv.at[c],
            device_id={"ep": behind(c, 1, 0), "hid": hid}, device_id_type=pl.DeviceIdType.MESH,
        )

    att = att_ref[...]
    loads[0].wait()
    for j in range(HID):
        proj[j] = dot(att, ow_v[:, cols(j)]).astype(BF)
    pl.semaphore_wait(barrier, EXPERTS - 1 + HID - 1)
    for j in (2, 1, 3):
        p_copy(j).start()

    row = lax.broadcasted_iota(jnp.int32, (rows, tok), 0)
    number = row // MOST
    near = (number // 8) ^ 1
    far = jnp.where(number // 8 == 1, 4, 8 - near)
    step = jnp.where((number // 4) % 2 == 0, near, far)
    expert = (
        16 * ((why + (number % 4) // 2) % 2) + 2 * ((zed + step) % 8) + (core + number) % 2
    )
    place = (row % MOST).astype(F32)
    named = jnp.zeros((rows, tok), F32)
    weight = jnp.zeros((rows, tok), F32)
    for k in range(routes_ref.shape[0]):
        same = routes_ref[k : k + 1, :] == expert
        named = named + jnp.where(same, 1.0, 0.0)
        weight = weight + jnp.where(same, rw_ref[k : k + 1, :], 0.0)
    earlier = jnp.where(
        lax.broadcasted_iota(jnp.int32, (tok, tok), 0)
        < lax.broadcasted_iota(jnp.int32, (tok, tok), 1),
        1.0,
        0.0,
    ).astype(BF)
    rank = dot(named.astype(BF), earlier)
    hit = jnp.where(rank == place, named, 0.0)
    pick = hit.astype(BF)
    scaled = (hit * weight).T
    high = scaled.astype(BF)
    low = (scaled - high.astype(F32)).astype(BF)

    total = proj[0].astype(F32)
    for j in range(1, HID):
        p_copy(j).wait_recv()
        total = total + projr[j].astype(F32)
    mixed = (stream_ref[...].astype(F32) + total.astype(BF).astype(F32)).astype(BF)

    for c in range(CHUNKS):
        block = dot(pick[c * crows : (c + 1) * crows], mixed).astype(BF)
        outg[chunk(c)] = block
        if c == 1:
            full[0, own] = block[0:MOST]
        each(c, lambda *n: d_copy(*n).start())

    def gather(c):
        d_all(c).wait_recv()
        for j in (1, 3):
            f_copy(j, c).start()

    def gather_on(c):
        for b in range(2):
            f_copy(1 + 2 * b, c).wait_recv()
            f_pass(b, c).start()

    def compute(c):
        gate = jnp.zeros((crows, width), F32)
        up = jnp.zeros((crows, width), F32)
        for j in (0, 1, 3, 2):
            if j == 2:
                f_pass(0, c).wait_recv()
                f_pass(1, c).wait_recv()
            features = full[j, chunk(c)]
            gate = gate + dot_t(features, gu_v[:width, cols(j)])
            up = up + dot_t(features, gu_v[width:, cols(j)])
        hidden = (jnp.maximum(gate, 0.0) * up).astype(BF)
        part[2, chunk(c)] = dot(hidden, down_v[:, cols(2)]).astype(BF)
        for b in range(2):
            s_pass(b, c).start()
        for j in (1, 3):
            part[j, chunk(c)] = dot(hidden, down_v[:, cols(j)]).astype(BF)
            s_copy(j, (3 - j) // 2, c).start()
        part[0, chunk(c)] = dot(hidden, down_v[:, cols(0)]).astype(BF)

    def sum_on(c):
        for b in range(2):
            j = 1 + 2 * b
            s_pass(b, c).wait_recv()
            both = part[j, half(c, b)].astype(F32) + passing[half(c, b)].astype(F32)
            part[j, half(c, b)] = both.astype(BF)
            s_copy(j, b, c).start()

    def give_back(c):
        for j in (1, 3):
            for b in range(2):
                s_copy(j, b, c).wait_recv()
        value = part[0, chunk(c)].astype(F32) + partr[0, chunk(c)].astype(F32)
        value = (value + partr[1, chunk(c)].astype(F32)).astype(BF)
        res[chunk(c)] = value
        if c == 1:
            ret[own] = value[0:MOST]
        each(c, lambda *n: r_copy(*n).start())

    gather(0)
    for n in range(1, 3):
        loads[n].wait()
    gather_on(0)
    gather(1)
    compute(0)
    gather_on(1)
    gather(2)
    sum_on(0)
    compute(1)
    gather_on(2)
    gather(3)
    give_back(0)
    sum_on(1)
    compute(2)
    gather_on(3)
    give_back(1)
    sum_on(2)
    compute(3)
    give_back(2)
    sum_on(3)
    give_back(3)

    mixture = jnp.zeros((tok, quarter), F32)
    for c in range(CHUNKS):
        r_all(c).wait_recv()
        back = ret[chunk(c)]
        mixture = mixture + dot(high[:, c * crows : (c + 1) * crows], back)
        mixture = mixture + dot(low[:, c * crows : (c + 1) * crows], back)
    residual = mixed.astype(F32) + mixture
    residual_ref[...] = residual
    squares = residual * residual
    lanes = squares[:, 0:128]
    for n in range(1, quarter // 128):
        lanes = lanes + squares[:, n * 128 : (n + 1) * 128]
    sq[0] = lanes
    for j in (2, 1, 3):
        q_copy(j).start()

    for j in range(1, HID):
        p_copy(j).wait_send()
    for c in range(CHUNKS):
        for b in range(2):
            f_copy(1 + 2 * b, c).wait_send()
            f_pass(b, c).wait_send()
            s_pass(b, c).wait_send()
            s_copy(1, b, c).wait_send()
            s_copy(3, b, c).wait_send()
    for c in range(CHUNKS):
        d_all(c).wait_send()
        r_all(c).wait_send()

    for j in range(1, HID):
        q_copy(j).wait_recv()
        lanes = lanes + sq[j]
    rms = jnp.sum(lanes, axis=1, keepdims=True) / (quarter * HID)
    inverse_ref[...] = jnp.broadcast_to(lax.rsqrt(rms + EPSILON), residual.shape)
    for j in range(1, HID):
        q_copy(j).wait_send()


def on_device(attention, stream, o_weight, routes, route_weight, gate_up, down_proj, norm_gain):
    tok, quarter = stream.shape
    full_width = quarter * HID
    width = gate_up.shape[3]
    rows = EXPERTS * MOST
    gate_up_t = gate_up[0].transpose(1, 2, 0).reshape(2 * width, full_width)
    down = down_proj[0]
    vmem = pl.BlockSpec(memory_space=pltpu.VMEM)
    hbm = pl.BlockSpec(memory_space=pl.ANY)
    dma = pltpu.SemaphoreType.DMA
    residual, inverse = pl.pallas_call(
        kernel,
        out_shape=(
            jax.ShapeDtypeStruct((tok, quarter), F32),
            jax.ShapeDtypeStruct((tok, quarter), F32),
        ),
        in_specs=[vmem] * 4 + [hbm] * 3,
        out_specs=(vmem, vmem),
        scratch_shapes=[
            pltpu.VMEM(o_weight.shape, BF),
            pltpu.VMEM(gate_up_t.shape, BF),
            pltpu.VMEM(down.shape, BF),
            pltpu.VMEM((HID, tok, quarter), BF),
            pltpu.VMEM((HID, tok, quarter), BF),
            pltpu.VMEM((rows, quarter), BF),
            pltpu.VMEM((HID, rows, quarter), BF),
            pltpu.VMEM((HID, rows, quarter), BF),
            pltpu.VMEM((2, rows, quarter), BF),
            pltpu.VMEM((rows, quarter), BF),
            pltpu.VMEM((rows, quarter), BF),
            pltpu.VMEM((rows, quarter), BF),
            pltpu.VMEM((HID, tok, 128), F32),
            dma((3,)),
            dma((HID,)), dma((HID,)),
            dma((CHUNKS,)), dma((CHUNKS,)),
            dma((HID, CHUNKS)), dma((HID, CHUNKS)),
            dma((3, 2, CHUNKS)), dma((3, 2, CHUNKS)),
            dma((CHUNKS,)), dma((CHUNKS,)),
            dma((HID,)), dma((HID,)),
        ],
        compiler_params=pltpu.CompilerParams(collective_id=0, has_side_effects=True),
    )(attention, stream, routes.T, route_weight.T, o_weight, gate_up_t, down)
    normed = (residual * inverse * norm_gain[None, :]).astype(BF)
    return residual.astype(BF), normed


def solution(mesh):
    in_specs = (
        P("ep", "hid"),
        P("ep", "hid"),
        P("hid", None),
        P("ep", None),
        P("ep", None),
        P("ep", None, None, "hid"),
        P("ep", "hid", None),
        P("hid"),
    )
    out_specs = (P("ep", "hid"), P("ep", "hid"))
    return jax.shard_map(
        on_device, mesh=mesh, in_specs=in_specs, out_specs=out_specs, check_vma=False
    )
```

```python
import jax
import jax.numpy as jnp
from jax import lax
from jax.experimental import pallas as pl
from jax.experimental.pallas import tpu as pltpu
from jax.sharding import PartitionSpec as P

EXPERTS = 32
MOST = 16
HID = 4
CHUNKS = 4
EPSILON = 1e-06
BF = jnp.bfloat16
F32 = jnp.float32


def dot(a, b):
    return jnp.dot(a, b, preferred_element_type=F32)


def dot_t(a, b):
    return lax.dot_general(a, b, (((1,), (1,)), ((), ())), preferred_element_type=F32)


def kernel(
    att_ref, stream_ref, routes_ref, rw_ref, ow_hbm, gu_hbm, down_hbm,
    residual_ref, inverse_ref,
    ow_v, gu_v, down_v, proj, projr, outg, full, part, partr, passing, res, ret, sq,
    w_sem, p_send, p_recv, d_send, d_recv, f_send, f_recv, s_send, s_recv, r_send, r_recv,
    q_send, q_recv,
):
    me = lax.axis_index("ep")
    hid = lax.axis_index("hid")
    loc = lax.rem(me, EXPERTS)
    base = me - loc
    tok, quarter = stream_ref.shape
    rows = EXPERTS * MOST
    crows = rows // CHUNKS
    hrows = crows // 2
    width = gu_v.shape[0] // 2

    core, zed, why = lax.rem(loc, 2), lax.rem(loc // 2, 8), loc // 16

    def distance(c, b):
        near = (1, 0, 3, 2)[c]
        return near if b == 0 else (4 if c == 1 else 8 - near)

    def ahead(c, b, q):
        return (
            base + 16 * lax.rem(why + q // 2, 2) + 2 * lax.rem(zed + distance(c, b), 8)
            + lax.rem(core + q % 2, 2)
        )

    def behind(c, b, q):
        return (
            base + 16 * lax.rem(why + q // 2, 2) + 2 * lax.rem(zed + 8 - distance(c, b), 8)
            + lax.rem(core + q % 2, 2)
        )

    def hid_up(j):
        return lax.rem(hid + j, HID)

    def cols(j):
        return pl.ds(pl.multiple_of(hid_up(j) * quarter, quarter), quarter)

    def slot(i):
        return pl.ds(i * MOST, MOST)

    def chunk(c):
        return pl.ds(c * crows, crows)

    def half(c, b):
        return pl.ds(c * crows + b * hrows, hrows)

    loads = [
        pltpu.make_async_copy(src, dst, w_sem.at[n])
        for n, (src, dst) in enumerate(
            [(ow_hbm, ow_v), (gu_hbm, gu_v), (down_hbm, down_v)]
        )
    ]
    for load in loads:
        load.start()

    barrier = pltpu.get_barrier_semaphore()

    def greet(i, carry):
        pl.semaphore_signal(
            barrier, inc=1, device_id={"ep": base + lax.rem(loc + i, EXPERTS), "hid": hid},
            device_id_type=pl.DeviceIdType.MESH,
        )
        return carry

    lax.fori_loop(1, EXPERTS, greet, 0)
    for j in range(1, HID):
        pl.semaphore_signal(
            barrier, inc=1, device_id={"ep": me, "hid": hid_up(j)},
            device_id_type=pl.DeviceIdType.MESH,
        )

    def over_hid(src, dst, send, recv, j):
        return pltpu.make_async_remote_copy(
            src_ref=src, dst_ref=dst, send_sem=send, recv_sem=recv,
            device_id={"ep": me, "hid": hid_up(j)}, device_id_type=pl.DeviceIdType.MESH,
        )

    def p_copy(j):
        return over_hid(proj.at[j], projr.at[j], p_send.at[j], p_recv.at[j], j)

    def f_copy(j, c):
        return pltpu.make_async_remote_copy(
            src_ref=full.at[0, chunk(c)], dst_ref=full.at[j, chunk(c)],
            send_sem=f_send.at[j, c], recv_sem=f_recv.at[j, c],
            device_id={"ep": me, "hid": hid_up(HID - j)}, device_id_type=pl.DeviceIdType.MESH,
        )

    def f_pass(b, c):
        j = 1 + 2 * b
        return pltpu.make_async_remote_copy(
            src_ref=full.at[j, half(c, b)], dst_ref=full.at[2, half(c, b)],
            send_sem=f_send.at[2 * b, c], recv_sem=f_recv.at[2 * b, c],
            device_id={"ep": me, "hid": hid_up(HID - j)}, device_id_type=pl.DeviceIdType.MESH,
        )

    def s_copy(j, b, c):
        return over_hid(
            part.at[j, half(c, b)], partr.at[j // 2, half(c, b)],
            s_send.at[j // 2, b, c], s_recv.at[j // 2, b, c], j
        )

    def s_pass(b, c):
        return over_hid(
            part.at[2, half(c, b)], passing.at[half(c, b)],
            s_send.at[2, b, c], s_recv.at[2, b, c], 1 + 2 * b
        )

    def q_copy(j):
        return over_hid(sq.at[0], sq.at[j], q_send.at[j], q_recv.at[j], j)

    def d_copy(c, b, q):
        n = c * 8 + b * 4 + q
        return pltpu.make_async_remote_copy(
            src_ref=outg.at[slot(n)], dst_ref=full.at[0, slot(n)],
            send_sem=d_send.at[c], recv_sem=d_recv.at[c],
            device_id={"ep": ahead(c, b, q), "hid": hid}, device_id_type=pl.DeviceIdType.MESH,
        )

    def r_copy(c, b, q):
        n = c * 8 + b * 4 + q
        return pltpu.make_async_remote_copy(
            src_ref=res.at[slot(n)], dst_ref=ret.at[slot(n)],
            send_sem=r_send.at[c], recv_sem=r_recv.at[c],
            device_id={"ep": behind(c, b, q), "hid": hid}, device_id_type=pl.DeviceIdType.MESH,
        )

    def each(c, act):
        for q in range(4):
            for b in range(2):
                if (c, b, q) != (1, 0, 0):
                    act(c, b, q)

    own = pl.ds(crows, MOST)

    def d_all(c):
        part_rows = pl.ds(c * crows, crows - MOST if c == 1 else crows)
        return pltpu.make_async_remote_copy(
            src_ref=outg.at[part_rows], dst_ref=full.at[0, part_rows],
            send_sem=d_send.at[c], recv_sem=d_recv.at[c],
            device_id={"ep": ahead(c, 1, 0), "hid": hid}, device_id_type=pl.DeviceIdType.MESH,
        )

    def r_all(c):
        part_rows = pl.ds(c * crows, crows - MOST if c == 1 else crows)
        return pltpu.make_async_remote_copy(
            src_ref=res.at[part_rows], dst_ref=ret.at[part_rows],
            send_sem=r_send.at[c], recv_sem=r_recv.at[c],
            device_id={"ep": behind(c, 1, 0), "hid": hid}, device_id_type=pl.DeviceIdType.MESH,
        )

    att = att_ref[...]
    loads[0].wait()
    for j in range(HID):
        proj[j] = dot(att, ow_v[:, cols(j)]).astype(BF)
    pl.semaphore_wait(barrier, EXPERTS - 1 + HID - 1)
    for j in (2, 1, 3):
        p_copy(j).start()

    row = lax.broadcasted_iota(jnp.int32, (rows, tok), 0)
    number = row // MOST
    near = (number // 8) ^ 1
    far = jnp.where(number // 8 == 1, 4, 8 - near)
    step = jnp.where((number // 4) % 2 == 0, near, far)
    expert = (
        16 * ((why + (number % 4) // 2) % 2) + 2 * ((zed + step) % 8) + (core + number) % 2
    )
    place = (row % MOST).astype(F32)
    named = jnp.zeros((rows, tok), F32)
    weight = jnp.zeros((rows, tok), F32)
    for k in range(routes_ref.shape[0]):
        same = routes_ref[k : k + 1, :] == expert
        named = named + jnp.where(same, 1.0, 0.0)
        weight = weight + jnp.where(same, rw_ref[k : k + 1, :], 0.0)
    earlier = jnp.where(
        lax.broadcasted_iota(jnp.int32, (tok, tok), 0)
        < lax.broadcasted_iota(jnp.int32, (tok, tok), 1),
        1.0,
        0.0,
    ).astype(BF)
    rank = dot(named.astype(BF), earlier)
    hit = jnp.where(rank == place, named, 0.0)
    pick = hit.astype(BF)
    scaled = (hit * weight).T
    high = scaled.astype(BF)
    low = (scaled - high.astype(F32)).astype(BF)

    total = proj[0].astype(F32)
    for j in range(1, HID):
        p_copy(j).wait_recv()
        total = total + projr[j].astype(F32)
    mixed = (stream_ref[...].astype(F32) + total.astype(BF).astype(F32)).astype(BF)

    for c in range(CHUNKS):
        block = dot(pick[c * crows : (c + 1) * crows], mixed).astype(BF)
        outg[chunk(c)] = block
        if c == 1:
            full[0, own] = block[0:MOST]
        each(c, lambda *n: d_copy(*n).start())

    def gather(c):
        d_all(c).wait_recv()
        for j in (1, 3):
            f_copy(j, c).start()

    def gather_on(c):
        for b in range(2):
            f_copy(1 + 2 * b, c).wait_recv()
            f_pass(b, c).start()

    def compute(c):
        gate = jnp.zeros((crows, width), F32)
        up = jnp.zeros((crows, width), F32)
        for j in (0, 1, 3, 2):
            if j == 2:
                f_pass(0, c).wait_recv()
                f_pass(1, c).wait_recv()
            features = full[j, chunk(c)]
            gate = gate + dot_t(features, gu_v[:width, cols(j)])
            up = up + dot_t(features, gu_v[width:, cols(j)])
        hidden = (jnp.maximum(gate, 0.0) * up).astype(BF)
        part[2, chunk(c)] = dot(hidden, down_v[:, cols(2)]).astype(BF)
        for b in range(2):
            s_pass(b, c).start()
        for j in (1, 3):
            part[j, chunk(c)] = dot(hidden, down_v[:, cols(j)]).astype(BF)
            s_copy(j, (3 - j) // 2, c).start()
        part[0, chunk(c)] = dot(hidden, down_v[:, cols(0)]).astype(BF)

    def sum_on(c):
        for b in range(2):
            j = 1 + 2 * b
            s_pass(b, c).wait_recv()
            both = part[j, half(c, b)].astype(F32) + passing[half(c, b)].astype(F32)
            part[j, half(c, b)] = both.astype(BF)
            s_copy(j, b, c).start()

    def give_back(c):
        for j in (1, 3):
            for b in range(2):
                s_copy(j, b, c).wait_recv()
        value = part[0, chunk(c)].astype(F32) + partr[0, chunk(c)].astype(F32)
        value = (value + partr[1, chunk(c)].astype(F32)).astype(BF)
        res[chunk(c)] = value
        if c == 1:
            ret[own] = value[0:MOST]
        each(c, lambda *n: r_copy(*n).start())

    gather(0)
    for n in range(1, 3):
        loads[n].wait()
    gather_on(0)
    gather(1)
    compute(0)
    gather_on(1)
    gather(2)
    sum_on(0)
    compute(1)
    gather_on(2)
    gather(3)
    give_back(0)
    sum_on(1)
    compute(2)
    gather_on(3)
    give_back(1)
    sum_on(2)
    compute(3)
    give_back(2)
    sum_on(3)
    give_back(3)

    mixture = jnp.zeros((tok, quarter), F32)
    for c in range(CHUNKS):
        r_all(c).wait_recv()
        back = ret[chunk(c)]
        mixture = mixture + dot(high[:, c * crows : (c + 1) * crows], back)
        mixture = mixture + dot(low[:, c * crows : (c + 1) * crows], back)
    residual = mixed.astype(F32) + mixture
    residual_ref[...] = residual
    squares = residual * residual
    sums = jnp.broadcast_to(jnp.sum(squares, axis=1, keepdims=True), (tok, 128))
    sums = jnp.concatenate([sums] * (128 // tok), axis=0).T[0:8]
    sq[0] = sums
    for j in (2, 1, 3):
        q_copy(j).start()

    for j in range(1, HID):
        p_copy(j).wait_send()
    for c in range(CHUNKS):
        for b in range(2):
            f_copy(1 + 2 * b, c).wait_send()
            f_pass(b, c).wait_send()
            s_pass(b, c).wait_send()
            s_copy(1, b, c).wait_send()
            s_copy(3, b, c).wait_send()
    for c in range(CHUNKS):
        d_all(c).wait_send()
        r_all(c).wait_send()

    for j in range(1, HID):
        q_copy(j).wait_recv()
        sums = sums + sq[j]
    rms = sums.T[0:tok, 0:1] / (quarter * HID)
    inverse_ref[...] = jnp.broadcast_to(lax.rsqrt(rms + EPSILON), residual.shape)
    for j in range(1, HID):
        q_copy(j).wait_send()


def on_device(attention, stream, o_weight, routes, route_weight, gate_up, down_proj, norm_gain):
    tok, quarter = stream.shape
    full_width = quarter * HID
    width = gate_up.shape[3]
    rows = EXPERTS * MOST
    gate_up_t = gate_up[0].transpose(1, 2, 0).reshape(2 * width, full_width)
    down = down_proj[0]
    vmem = pl.BlockSpec(memory_space=pltpu.VMEM)
    hbm = pl.BlockSpec(memory_space=pl.ANY)
    dma = pltpu.SemaphoreType.DMA
    residual, inverse = pl.pallas_call(
        kernel,
        out_shape=(
            jax.ShapeDtypeStruct((tok, quarter), F32),
            jax.ShapeDtypeStruct((tok, quarter), F32),
        ),
        in_specs=[vmem] * 4 + [hbm] * 3,
        out_specs=(vmem, vmem),
        scratch_shapes=[
            pltpu.VMEM(o_weight.shape, BF),
            pltpu.VMEM(gate_up_t.shape, BF),
            pltpu.VMEM(down.shape, BF),
            pltpu.VMEM((HID, tok, quarter), BF),
            pltpu.VMEM((HID, tok, quarter), BF),
            pltpu.VMEM((rows, quarter), BF),
            pltpu.VMEM((HID, rows, quarter), BF),
            pltpu.VMEM((HID, rows, quarter), BF),
            pltpu.VMEM((2, rows, quarter), BF),
            pltpu.VMEM((rows, quarter), BF),
            pltpu.VMEM((rows, quarter), BF),
            pltpu.VMEM((rows, quarter), BF),
            pltpu.VMEM((HID, 8, 128), F32),
            dma((3,)),
            dma((HID,)), dma((HID,)),
            dma((CHUNKS,)), dma((CHUNKS,)),
            dma((HID, CHUNKS)), dma((HID, CHUNKS)),
            dma((3, 2, CHUNKS)), dma((3, 2, CHUNKS)),
            dma((CHUNKS,)), dma((CHUNKS,)),
            dma((HID,)), dma((HID,)),
        ],
        compiler_params=pltpu.CompilerParams(collective_id=0, has_side_effects=True),
    )(attention, stream, routes.T, route_weight.T, o_weight, gate_up_t, down)
    normed = (residual * inverse * norm_gain[None, :]).astype(BF)
    return residual.astype(BF), normed


def solution(mesh):
    in_specs = (
        P("ep", "hid"),
        P("ep", "hid"),
        P("hid", None),
        P("ep", None),
        P("ep", None),
        P("ep", None, None, "hid"),
        P("ep", "hid", None),
        P("hid"),
    )
    out_specs = (P("ep", "hid"), P("ep", "hid"))
    return jax.shard_map(
        on_device, mesh=mesh, in_specs=in_specs, out_specs=out_specs, check_vma=False
    )
```
